128 devices in a mesh: row: 8 (over y_hi, x), col: 16 (over y_lo, z, core).
Axes of the slice: x: 4, y: 4 (y_hi: 2, y_lo: 2; y = y_hi * 2 + y_lo), z: 4, core: 2. Of those that a mesh axis runs over, the one named last changes fastest.
Arguments:
- slip_log: float32 [512, 32768], P(None, ('row', 'col')), may hold values from -2.5 to 2.5
- fault_state: float32 [512, 32768], P(None, ('row', 'col')), may hold values from -2.5 to 2.5
- direct_effect: float32 [512, 32768], P(None, ('row', 'col')), may hold values from 0.3 to 1
- loading: float32 [512, 32768], P(None, ('row', 'col')), may hold values from 0.5 to 1.5
- dense_near: bfloat16 [32, 3, 1024, 1024], P('row', None, 'col'), may hold values from -0.109375 to 0.109375
- low_left: bfloat16 [32, 32, 32, 1024], P('row', 'col'), may hold values from -1 to 1
- low_right: bfloat16 [32, 32, 32, 1024], P('row', 'col'), may hold values from -0.03125 to 0.03125
- block_ranks: int32 [32, 32], P('row', 'col'), may hold values from 8 to 32
Outputs:
- new_log: float32 [512, 32768], P(None, ('row', 'col'))
- new_state: float32 [512, 32768], P(None, ('row', 'col'))
The draws below stay inside these ranges and needn't reach their ends.
Inputs may be any that keep to these rules, and one draw needn't show every extreme that they name: `block_ranks`: only factor pairs below this count take part in a far block; entries of near blocks are not read.
All inputs are finite; a program needn't handle non-finite values.
Results may differ from the reference program's by a relative error of at most 0.0016.
Values may be sent and summed in bfloat16 or wider, within the bound.
No kernel may reach another device: no remote copies, remote signals or barrier semaphores. Data moves between devices by JAX's collectives and lax.ppermute only.
A program may use at most 128 MiB of HBM per device.

```python
import math
import jax
import jax.numpy as jnp
from jax import lax

LEAF = 1024
RANK = 32
MEMBERS = 512
BLOCKS = 32
CELLS = 32768


def plant(drawn, own_key, least, largest):
    shape = drawn.shape
    place = [jax.random.randint(jax.random.fold_in(own_key, axis), (), 0, shape[axis]) for axis in range(len(shape))]
    drawn = drawn.at[tuple(place)].set(least)
    longest = shape.index(max(shape))
    place[longest] = (place[longest] + 1) % shape[longest]
    return drawn.at[tuple(place)].set(largest)


def level_of(key, extent, cuts, low, high):
    factor_of = 1.0
    for position, shards_of in cuts:
        draws = jax.random.uniform(jax.random.fold_in(jax.random.fold_in(key, 6), position), (shards_of,), jnp.float32, low / len(cuts), high / len(cuts))
        factor_of = factor_of * jnp.repeat(jnp.exp(draws), extent[position] // shards_of).reshape((-1,) + (1,) * (len(extent) - 1 - position))
    return factor_of


def normal_values(own_key, extent, spread, bound, shards=(), kind=jnp.bfloat16):
    loudness = level_of(own_key, extent, shards, -0.22, 0.18) if shards else 1.0
    values = jax.random.normal(own_key, extent, jnp.float32) * spread * loudness
    return jnp.minimum(jnp.maximum(values, -bound), bound).astype(kind)


def setup_inputs(seed: int = 0) -> dict:
    seeds = jax.random.split(jax.random.key(seed), 9)
    slip_log = normal_values(seeds[0], (MEMBERS, CELLS), 0.5, 2.5, ((1, 128),), jnp.float32)
    fault_state = normal_values(seeds[1], (MEMBERS, CELLS), 0.5, 2.5, ((1, 128),), jnp.float32)
    direct_effect = jnp.clip(jnp.exp(math.log(1.0) - 1.2039728 * jax.random.uniform(seeds[2], (MEMBERS, CELLS), jnp.float32) ** level_of(seeds[2], (MEMBERS, CELLS), ((1, 128),), -0.2, 0.2)), 0.3, 1.0)
    loading = jnp.clip(0.5 + 1.0 * jax.random.uniform(seeds[3], (MEMBERS, CELLS), jnp.float32) ** level_of(seeds[3], (MEMBERS, CELLS), ((1, 128),), -0.2, 0.2), 0.5, 1.5)
    dense_near = normal_values(seeds[4], (BLOCKS, 3, LEAF, LEAF), (3 * LEAF) ** -0.5, 0.109375, ((0, 8), (2, 16)))
    low_left = normal_values(seeds[5], (BLOCKS, BLOCKS, RANK, LEAF), RANK ** -0.5, 1.0, ((0, 8), (1, 16)))
    low_right = normal_values(seeds[6], (BLOCKS, BLOCKS, RANK, LEAF), CELLS ** -0.5, 0.03125, ((0, 8), (1, 16)))
    block_ranks = plant(jax.random.randint(seeds[7], (BLOCKS, BLOCKS), RANK // 4, RANK + 1), jax.random.fold_in(seeds[7], 1), RANK // 4, RANK).astype(jnp.int32)
    return dict(slip_log=slip_log, fault_state=fault_state, direct_effect=direct_effect, loading=loading, dense_near=dense_near, low_left=low_left, low_right=low_right, block_ranks=block_ranks)


step_length = 0.25
damping = 0.5


def friction_rates(log_rate, state_var, effect, load, traction):
    velocity = jnp.exp(log_rate)
    state_rate = jnp.exp(-state_var) - velocity
    log_change = (load - traction - state_rate) / (effect + damping * velocity)
    return log_change, state_rate


def operator_apply(slip_bf, dense_near, low_left, low_right, block_ranks):
    columns = slip_bf.astype(jnp.float32).reshape(MEMBERS, BLOCKS, LEAF)
    levels = jnp.arange(RANK, dtype=jnp.int32)
    window = jnp.stack([jnp.roll(columns, 1, axis=1), columns, jnp.roll(columns, -1, axis=1)], axis=2)
    window = jnp.transpose(window, (1, 0, 2, 3))
    block_ids = jnp.arange(BLOCKS, dtype=jnp.int32)

    def one_row(packed):
        row_id, near_row, win_row, left_row, right_row, rank_row = packed
        near_sum = jnp.einsum("eol,oil->ei", win_row, near_row.astype(jnp.float32))
        diff = jnp.abs(block_ids - row_id)
        far_mask = jnp.minimum(diff, BLOCKS - diff) > 1
        keep = ((levels[None, :] < rank_row[:, None]) & far_mask[:, None]).astype(jnp.float32)
        coeffs = jnp.einsum("ecj,ckj->eck", columns, right_row.astype(jnp.float32)) * keep[None]
        coeffs = lax.optimization_barrier(coeffs.astype(jnp.bfloat16)).astype(jnp.float32)
        far_sum = jnp.einsum("eck,cki->ei", coeffs, left_row.astype(jnp.float32))
        return near_sum + far_sum

    rows = lax.map(one_row, (block_ids, dense_near, window, low_left, low_right, block_ranks))
    return jnp.transpose(rows, (1, 0, 2)).reshape(MEMBERS, CELLS)


def reference(slip_log, fault_state, direct_effect, loading, dense_near, low_left, low_right, block_ranks):
    def section(log_rate, state_var):
        slip_bf = jnp.exp(log_rate).astype(jnp.bfloat16)
        traction = operator_apply(slip_bf, dense_near, low_left, low_right, block_ranks)
        return friction_rates(log_rate, state_var, direct_effect, loading, traction)

    first_log, first_state = section(slip_log, fault_state)
    mid_log = slip_log + step_length * first_log
    mid_state = fault_state + step_length * first_state
    second_log, second_state = section(mid_log, mid_state)
    new_log = slip_log + 0.5 * step_length * (first_log + second_log)
    new_state = fault_state + 0.5 * step_length * (first_state + second_state)
    return new_log, new_state
```

```python
import functools
import jax
import jax.numpy as jnp
from jax import lax
from jax.experimental import pallas as pl
from jax.experimental.pallas import tpu as pltpu
from jax.sharding import PartitionSpec as P

step_length = 0.25
damping = 0.5
ALL = ("row", "col")
F32 = jnp.float32
BF16 = jnp.bfloat16
NT = (((1,), (1,)), ((), ()))
TN = (((0,), (0,)), ((), ()))


def pick(array, index, axis=0):
    return lax.dynamic_index_in_dim(array, index, axis, keepdims=False)


def moved(value, target, count):
    return lax.ppermute(value, ALL, [(d, target(d)) for d in range(count)])


def coeff_kernel(where_ref, right_ref, s0, s1, s2, s3, out_ref):
    q = where_ref[0]
    total = None
    for t, piece in enumerate((s0, s1, s2, s3)):
        start = pl.multiple_of((q ^ t) * 256, 256)
        term = lax.dot_general(
            right_ref[:, pl.ds(start, 256)], piece[...], NT, preferred_element_type=F32
        )
        total = term if total is None else total + term
    blocks = total.reshape(32, 8, 512).astype(BF16)
    for zl in range(2):
        for core in range(2):
            out_ref[:, zl, core] = blocks[:, :, core * 256 : core * 256 + 256]


def coefficients(where, right, pieces):
    return pl.pallas_call(
        coeff_kernel,
        out_shape=jax.ShapeDtypeStruct((32, 2, 2, 8, 256), BF16),
        in_specs=[pl.BlockSpec(memory_space=pltpu.SMEM)] + [pl.BlockSpec(memory_space=pltpu.VMEM)] * 5,
        out_specs=pl.BlockSpec(memory_space=pltpu.VMEM),
        name="coeff",
    )(where, right, *pieces)


def traction_of(where_ref, pieces, own_ref, other_ref, near_ref, left_ref, acc_ref):
    q = where_ref[0]

    @pl.when(pl.program_id(0) == 0)
    def _():
        acc_ref[...] = lax.dot_general(own_ref[...], left_ref[...], TN, preferred_element_type=F32)

    @pl.when(pl.program_id(0) == 1)
    def _():
        acc_ref[...] = lax.dot_general(other_ref[...], left_ref[...], TN, preferred_element_type=F32)

    total = acc_ref[...]
    for o in range(3):
        for t in range(4):
            start = pl.multiple_of((q ^ t) * 256, 256)
            total = total + lax.dot_general(
                pieces[o * 4 + t][...], near_ref[o, :, pl.ds(start, 256)], NT, preferred_element_type=F32
            )
    return total


def rates(log_rate, state, effect, load, traction):
    velocity = jnp.exp(log_rate)
    state_rate = jnp.exp(-state) - velocity
    log_change = (load - traction - state_rate) / (effect + damping * velocity)
    return log_change, state_rate


def first_kernel(where_ref, *refs):
    pieces, (own, other, near, left, log, state, effect, load) = refs[:12], refs[12:20]
    mid_log, mid_state, sum_log, sum_state, slip, acc = refs[20:]
    traction = traction_of(where_ref, pieces, own, other, near, left, acc)
    log_now, state_now = log[...], state[...]
    dl, dp = rates(log_now, state_now, effect[...], load[...], traction)
    middle = log_now + step_length * dl
    mid_log[...] = middle
    mid_state[...] = state_now + step_length * dp
    sum_log[...] = log_now + 0.5 * step_length * dl
    sum_state[...] = state_now + 0.5 * step_length * dp
    slip[...] = jnp.exp(middle).astype(BF16)


def second_kernel(where_ref, *refs):
    pieces, (own, other, near, left, log, state, effect, load, sum_log, sum_state) = refs[:12], refs[12:22]
    new_log, new_state, acc = refs[22:]
    traction = traction_of(where_ref, pieces, own, other, near, left, acc)
    dl, dp = rates(log[...], state[...], effect[...], load[...], traction)
    new_log[...] = sum_log[...] + 0.5 * step_length * dl
    new_state[...] = sum_state[...] + 0.5 * step_length * dp


def section_call(kernel, where, pieces, own, other, near, left, states, outs, name):
    members = pl.BlockSpec((256, 256), lambda h, w: (h ^ w[1], 0))
    whole2 = pl.BlockSpec((1024, 256), lambda h, w: (0, 0))
    whole3 = pl.BlockSpec((3, 256, 1024), lambda h, w: (0, 0, 0))
    return pl.pallas_call(
        kernel,
        grid_spec=pltpu.PrefetchScalarGridSpec(
            num_scalar_prefetch=1,
            grid=(2,),
            in_specs=[members] * 12 + [whole2, whole2, whole3, whole2] + [members] * len(states),
            out_specs=[members] * len(outs),
            scratch_shapes=[pltpu.VMEM((256, 256), F32)],
        ),
        out_shape=[jax.ShapeDtypeStruct((512, 256), d) for d in outs],
        name=name,
    )(where, *pieces, own, other, near, left, *states)


def on_device(
    slip_log, fault_state, direct_effect, loading, dense_near, low_left, low_right, block_ranks
):
    row = lax.axis_index("row")
    col = lax.axis_index("col")
    count = lax.axis_size("row") * lax.axis_size("col")
    block, quarter = col // 4, col % 4
    core = col % 2
    where = jnp.stack([quarter, core]).astype(jnp.int32)
    move = functools.partial(moved, count=count)

    levels = jnp.arange(32, dtype=jnp.int32)
    rows_of = row * 4 + jnp.arange(4, dtype=jnp.int32)
    cols_of = col * 2 + jnp.arange(2, dtype=jnp.int32)
    distance = jnp.abs(rows_of[:, None] - cols_of[None, :])
    far = jnp.minimum(distance, 32 - distance) > 1
    keep = (levels < block_ranks[:, :, None]) & far[:, :, None]
    masked = jnp.where(keep[..., None], low_right, 0).astype(BF16)
    halves = masked.reshape(4, 2, 2, 16, 1024)

    def right_target(d, t):
        r, c = d // 16, d % 16
        return (c // 2) * 16 + (c % 2) * 8 + (r ^ (t * 2))

    arrived = []
    for t in range(4):
        sent = lax.dynamic_slice(
            halves, (0, (row // 4) ^ (t // 2), ((row // 2) % 2) ^ (t % 2), 0, 0), (4, 1, 1, 16, 1024)
        ).reshape(4, 2, 8, 1024)
        arrived.append(move(sent, functools.partial(right_target, t=t)))
    kept = [pick(a, core, 1) for a in arrived]
    given = jnp.stack([pick(a, 1 - core, 1) for a in arrived])
    got = move(given, lambda d: d ^ 1)
    parts = [x for t in range(4) for x in (kept[t], got[t])]
    stacked = jnp.stack(parts)
    right = jnp.concatenate([pick(stacked, r ^ (col % 8)) for r in range(8)]).reshape(256, 1024)

    def near_target(d, s):
        r, a, q = d // 16, (d % 16) // 4, d % 4
        return r * 16 + (q ^ s) * 4 + a

    near_parts = jnp.stack(
        [move(pick(dense_near, quarter ^ s), functools.partial(near_target, s=s)) for s in range(4)]
    )
    near = jnp.concatenate([pick(near_parts, block ^ p) for p in range(4)], axis=1)

    left_out = low_left.reshape(4, 64, 4, 256).transpose(0, 2, 1, 3).reshape(16, 64, 256)
    left = lax.all_to_all(left_out, "col", 0, 0).reshape(1024, 256)

    def exchange(slip):
        zl = lambda d: d ^ 2
        partner = lambda d: d ^ 1
        own2 = move(slip, zl)
        before2 = move(slip, lambda d: ((d + 4) % count) ^ 2)
        after2 = move(slip, lambda d: ((d - 4) % count) ^ 2)
        own = [slip, move(slip, partner), own2, move(own2, partner)]
        sides = []
        for first in (before2, after2):
            second = move(first, zl)
            sides.append([second, move(second, partner), first, move(first, partner)])
        return sides[0] + own + sides[1], own

    def section(slip):
        pieces, own = exchange(slip)
        sent = coefficients(where, right, own).reshape(128, 8, 256)
        mine = lax.all_to_all(sent, ALL, 0, 0).reshape(1024, 256)
        return pieces, mine, move(mine, lambda d: d ^ 1)

    slip = jnp.exp(slip_log).astype(BF16)
    pieces, mine, other = section(slip)
    mid_log, mid_state, sum_log, sum_state, slip = section_call(
        first_kernel, where, pieces, mine, other, near, left,
        (slip_log, fault_state, direct_effect, loading), (F32, F32, F32, F32, BF16), "first",
    )
    pieces, mine, other = section(slip)
    return tuple(section_call(
        second_kernel, where, pieces, mine, other, near, left,
        (mid_log, mid_state, direct_effect, loading, sum_log, sum_state), (F32, F32), "second",
    ))


def solution(mesh):
    cells = P(None, ALL)
    in_specs = (
        cells, cells, cells, cells,
        P("row", None, "col", None), P("row", "col", None, None), P("row", "col", None, None), P("row", "col"),
    )
    return jax.shard_map(
        on_device, mesh=mesh, in_specs=in_specs, out_specs=(cells, cells), check_vma=False
    )
```

```python
import functools
import jax
import jax.numpy as jnp
from jax import lax
from jax.experimental import pallas as pl
from jax.experimental.pallas import tpu as pltpu
from jax.sharding import Mesh, PartitionSpec as P

step_length = 0.25
damping = 0.5
ALL = ("row", "chip", "core")
F32 = jnp.float32
BF16 = jnp.bfloat16
COUNT = 128


def pick(array, index, axis=0):
    return lax.dynamic_index_in_dim(array, index, axis, keepdims=False)


def move(value, target):
    return lax.ppermute(value, ALL, [(d, target(d)) for d in range(COUNT)])


def dot(a, b):
    return jnp.dot(a, b, preferred_element_type=F32)


def shape(*dims, dtype=F32):
    return jax.ShapeDtypeStruct(dims, dtype)


STATE = shape(512, 256)
SLIP = shape(512, 256, dtype=BF16)
TURNED = shape(256, 256)
HALF = shape(256, 256, dtype=BF16)
LEFT = shape(512, 1024, dtype=BF16)
SENT = shape(32, 2, 16, 256, dtype=BF16)
RIGHT = shape(512, 1024, dtype=BF16)
NEAR = shape(3, 512, 1024, dtype=BF16)
SCALARS = pl.BlockSpec(memory_space=pltpu.SMEM)
VECTORS = pl.BlockSpec(memory_space=pltpu.VMEM)


def call(kernel, outs, where, operands, flops, scratch=()):
    return pl.pallas_call(
        kernel,
        out_shape=outs,
        in_specs=[SCALARS] + [VECTORS] * len(operands),
        out_specs=[VECTORS] * len(outs),
        scratch_shapes=scratch,
        cost_estimate=pl.CostEstimate(flops=flops, bytes_accessed=5 << 20, transcendentals=0),
    )(where, *operands)


def coefficients_of(right_ref, own, pair, out_ref):
    total = dot(right_ref[:, :512], own[...]) + dot(right_ref[:, 512:], pair[...])
    blocks = total.astype(BF16).reshape(32, 16, 256)
    out_ref[:, 0] = blocks
    out_ref[:, 1] = blocks


def coeff_kernel(where_ref, right_ref, own, pair, out_ref):
    coefficients_of(right_ref, own, pair, out_ref)


def coeff_first_kernel(where_ref, *refs):
    parts, own, pair, out_ref, right_ref = refs[:8], *refs[8:]
    quarter, core, x_at = where_ref[0], where_ref[1], where_ref[3]
    for b in range(2):
        for u in range(4):
            r = (b ^ core) * 4 + (u ^ x_at)
            for t in range(4):
                start = pl.multiple_of((quarter ^ t) * 256, 256)
                right_ref[pl.ds(pl.multiple_of(r * 64, 64), 64), t * 256 : t * 256 + 256] = parts[b * 4 + u][
                    :, pl.ds(start, 256)
                ]
    coefficients_of(right_ref, own, pair, out_ref)


def near_inner(pieces, near_ref, out_ref):
    own, pair, inner, outer = pieces
    total = dot(near_ref[1, :, :512], own[...]) + dot(near_ref[1, :, 512:], pair[...])
    total = total + dot(near_ref[0, :, 512:], inner[...])
    out_ref[...] = total + dot(near_ref[2, :, 512:], outer[...])


def near_first_kernel(where_ref, *refs):
    pieces, parts, num, (out_ref, near_ref) = refs[:6], refs[6:14], refs[14], refs[15:]
    quarter, block, odd = where_ref[0], where_ref[2], where_ref[4]
    for half in range(2):
        for s in range(4):
            rows = pl.ds(pl.multiple_of(half * 256 + (block ^ s) * 64, 64), 64)
            for side, o in enumerate((2 - 2 * odd, 1, 2 * odd)):
                for t in range(4):
                    start = pl.multiple_of((quarter ^ t) * 256, 256)
                    near_ref[side, rows, t * 256 : t * 256 + 256] = parts[half * 4 + s][o, :, pl.ds(start, 256)]
    own, pair, inner, outer, across, beyond = pieces
    total = None
    for side, (low, high) in enumerate(((across, inner), (own, pair), (beyond, outer))):
        term = dot(near_ref[side, :, :512], low[...]) + dot(near_ref[side, :, 512:], high[...])
        total = term if total is None else total + term
    out_ref[...] = num[...] - total


def near_kernel(where_ref, own, pair, inner, outer, near_ref, out_ref):
    near_inner((own, pair, inner, outer), near_ref, out_ref)


def left_kernel(where_ref, own, received, out_ref):
    out_ref[:256] = own[...].T
    out_ref[256:] = received[...].T


def raise_kernel(where_ref, log, own, theirs):
    own[...] = jnp.exp(log[pl.ds(pl.multiple_of(where_ref[1] * 256, 256), 256), :]).astype(BF16)
    theirs[...] = jnp.exp(log[pl.ds(pl.multiple_of(256 - where_ref[1] * 256, 256), 256), :]).astype(BF16)


def join_kernel(where_ref, own, received, out_ref):
    out_ref[:256] = own[...].T
    out_ref[256:] = received[...].T


def prepare_first_kernel(where_ref, *refs):
    whole, received, (log_ref, effect_ref, load_ref, num, den, mid_state, sum_state) = refs[:4], refs[4:8], refs[8:]
    mine = pl.ds(pl.multiple_of(where_ref[1] * 256, 256), 256)
    for half in range(2):
        rows = slice(half * 256, half * 256 + 256)
        log, state, effect, load = (
            (received[i][...] if half else whole[i][mine, :]).T for i in range(4)
        )
        velocity = jnp.exp(log)
        state_rate = jnp.exp(-state) - velocity
        log_ref[rows] = log
        effect_ref[rows] = effect
        load_ref[rows] = load
        num[rows] = load - state_rate
        den[rows] = effect + damping * velocity
        mid_state[rows] = state + step_length * state_rate
        sum_state[rows] = state + 0.5 * step_length * state_rate


def prepare_second_kernel(where_ref, log, state, effect, load, sum_state, num, den, own, other):
    place = pl.ds(pl.multiple_of(where_ref[1] * 256, 256), 256)
    for half in range(2):
        rows = slice(half * 256, half * 256 + 256)
        velocity = jnp.exp(log[rows])
        state_rate = jnp.exp(-state[rows]) - velocity
        num[rows] = load[rows] - state_rate
        den[rows] = effect[rows] + damping * velocity
        new_state = (sum_state[rows] + 0.5 * step_length * state_rate).T
        if half:
            other[...] = new_state
        else:
            own[place, :] = new_state


def near_outer_kernel(where_ref, num, partial, across, beyond, near_ref, out_ref):
    near = partial[...] + dot(near_ref[0, :, :512], across[...]) + dot(near_ref[2, :, :512], beyond[...])
    out_ref[...] = num[...] - near


def far_first_kernel(where_ref, coeff, left, num, den, log, mid_log, sum_log, slip):
    for half in range(2):
        rows = slice(half * 256, half * 256 + 256)
        change = (num[rows] - dot(left[rows], coeff[...])) / den[rows]
        middle = log[rows] + step_length * change
        mid_log[rows] = middle
        sum_log[rows] = log[rows] + 0.5 * step_length * change
        slip[rows] = jnp.exp(middle).astype(BF16)


def far_second_kernel(where_ref, coeff, left, num, den, sum_log, own, other):
    place = pl.ds(pl.multiple_of(where_ref[1] * 256, 256), 256)
    for half in (1, 0):
        rows = slice(half * 256, half * 256 + 256)
        change = (num[rows] - dot(left[rows], coeff[...])) / den[rows]
        result = (sum_log[rows] + 0.5 * step_length * change).T
        if half:
            other[...] = result
        else:
            own[place, :] = result


def on_device(
    slip_log, fault_state, direct_effect, loading, dense_near, low_left, low_right, block_ranks
):
    row, chip, core = (lax.axis_index(name) for name in ALL)
    col = chip * 2 + core
    block, quarter = col // 4, col % 4
    x_at, z_at = row % 4, chip % 4
    where = jnp.stack([quarter, core, block, x_at, block % 2]).astype(jnp.int32)
    partner = lambda d: d ^ 1
    zl = lambda d: d ^ 2

    fourths = low_right.reshape(4, 4, 16, 1024)
    along = [pick(fourths, z_at ^ t, 1) for t in range(4)]
    along = [along[0]] + [move(along[t], lambda d: d ^ (2 * t)) for t in range(1, 4)]

    def right_target(d, u):
        r, c = d // 16, d % 16
        return ((c // 8) * 4 + ((r % 4) ^ u)) * 16 + (c % 2) * 8 + (c // 2 % 4) * 2 + r // 4

    arrived = [
        move(lax.select_n(z_at ^ x_at ^ u, *along), functools.partial(right_target, u=u)).reshape(64, 1024)
        for u in range(4)
    ]
    right_parts = arrived + [move(arrived[u], partner) for u in range(4)]

    levels = jnp.arange(32, dtype=jnp.int32)
    rows_of = row * 4 + jnp.arange(4, dtype=jnp.int32)
    cols_of = col * 2 + jnp.arange(2, dtype=jnp.int32)
    distance = jnp.abs(rows_of[:, None] - cols_of[None, :])
    far = jnp.minimum(distance, 32 - distance) > 1
    keep = ((levels < block_ranks[:, :, None]) & far[:, :, None]).reshape(4, 1, 64, 1)
    left_out = low_left.reshape(4, 64, 4, 256).transpose(0, 2, 1, 3)
    left_out = jnp.where(keep, left_out, 0).astype(BF16).reshape(16, 64, 256)
    left = lax.all_to_all(left_out, ("chip", "core"), 0, 0).reshape(1024, 256)
    lefts = (left, move(left, partner))

    def near_target(d, s):
        r, a, q = d // 16, (d % 16) // 4, d % 4
        return r * 16 + (q ^ s) * 4 + a

    parts = [move(pick(dense_near, quarter ^ s), functools.partial(near_target, s=s)) for s in range(4)]
    parts = parts + [move(parts[s], partner) for s in range(4)]

    own, theirs = call(raise_kernel, [HALF, HALF], where, (slip_log,), 1)
    (slip,) = call(join_kernel, [SLIP], where, (own, move(theirs, partner)), 1)
    arrays = (slip_log, fault_state, direct_effect, loading)
    received = [move(lax.dynamic_slice_in_dim(v, (1 - core) * 256, 256, 0), partner) for v in arrays]

    def exchange(slip):
        pair = move(slip, zl)
        inner = move(slip, lambda d: d ^ 6)
        outer = move(slip, lambda d: ((d + 4 if d & 4 else d - 4) % COUNT) ^ 2)
        return (slip, pair, inner, outer), (move(pair, lambda d: d ^ 6), move(outer, zl))

    def all_to_all(sent):
        return lax.all_to_all(sent.reshape(64, 16, 256), ("row", "chip"), 0, 0).reshape(1024, 256)

    def restored(own, other):
        return lax.dynamic_update_slice(own, move(other, partner), ((1 - core) * 256, 0))

    pieces, crossed = exchange(slip)
    sent, right = call(coeff_first_kernel, [SENT, RIGHT], where, (*right_parts, *pieces[:2]), 1 << 28)
    coeff = all_to_all(sent)
    (left,) = call(left_kernel, [LEFT], where, lefts, 1 << 20)
    log, effect, load, num, den, mid_state, sum_state = call(
        prepare_first_kernel, [STATE] * 7, where, (*arrays, *received), 1
    )
    num, near = call(near_first_kernel, [STATE, NEAR], where, (*pieces, *crossed, *parts, num), 3 << 28)
    mid_log, sum_log, slip = call(far_first_kernel, [STATE, STATE, SLIP], where, (coeff, left, num, den, log), 1 << 28)

    pieces, crossed = exchange(slip)
    (sent,) = call(coeff_kernel, [SENT], where, (right, *pieces[:2]), 1 << 28)
    coeff = all_to_all(sent)
    (partial,) = call(near_kernel, [STATE], where, (*pieces, near), 2 << 28)
    num, den, own, other = call(
        prepare_second_kernel, [STATE, STATE, STATE, TURNED], where,
        (mid_log, mid_state, effect, load, sum_state), 1,
    )
    (num,) = call(near_outer_kernel, [STATE], where, (num, partial, *crossed, near), 1 << 28)
    new_state = restored(own, other)
    own, other = call(far_second_kernel, [STATE, TURNED], where, (coeff, left, num, den, sum_log), 1 << 28)
    return restored(own, other), new_state


def solution(mesh):
    chips = Mesh(mesh.devices.reshape(8, 8, 2), ALL)
    cells, columns = P(None, ALL), ("chip", "core")
    in_specs = (
        cells, cells, cells, cells,
        P("row", None, columns, None), P("row", columns, None, None), P("row", columns, None, None), P("row", columns),
    )
    return jax.shard_map(
        on_device, mesh=chips, in_specs=in_specs, out_specs=(cells, cells), check_vma=False
    )
```

```python
import functools
import jax
import jax.numpy as jnp
from jax import lax
from jax.experimental import pallas as pl
from jax.experimental.pallas import tpu as pltpu
from jax.sharding import Mesh, PartitionSpec as P

step_length = 0.25
damping = 0.5
ALL = ("row", "chip", "core")
F32 = jnp.float32
BF16 = jnp.bfloat16
COUNT = 128


def pick(array, index, axis=0):
    return lax.dynamic_index_in_dim(array, index, axis, keepdims=False)


def move(value, target):
    return lax.ppermute(value, ALL, [(d, target(d)) for d in range(COUNT)])


def dot(a, b):
    return jnp.dot(a, b, preferred_element_type=F32)


def shape(*dims, dtype=F32):
    return jax.ShapeDtypeStruct(dims, dtype)


STATE = shape(512, 256)
SLIP = shape(512, 256, dtype=BF16)
TURNED = shape(256, 256)
HALF = shape(256, 256, dtype=BF16)
LEFT = shape(512, 1024, dtype=BF16)
SENT = shape(32, 2, 16, 256, dtype=BF16)
RIGHT = shape(512, 1024, dtype=BF16)
NEAR = shape(3, 512, 1024, dtype=BF16)
SCALARS = pl.BlockSpec(memory_space=pltpu.SMEM)
VECTORS = pl.BlockSpec(memory_space=pltpu.VMEM)


SMALL = ("coeff", "near", "near_outer", "raise", "join")


def call(kernel, outs, where, operands, name, flops, scratch=()):
    return pl.pallas_call(
        kernel,
        out_shape=outs,
        in_specs=[SCALARS] + [VECTORS] * len(operands),
        out_specs=[VECTORS] * len(outs),
        scratch_shapes=scratch,
        compiler_params=pltpu.CompilerParams(vmem_limit_bytes=20 << 20) if name in SMALL else None,
        cost_estimate=pl.CostEstimate(flops=flops, bytes_accessed=5 << 20, transcendentals=0),
    )(where, *operands)


def coefficients_of(right_ref, own, pair, out_ref):
    total = dot(right_ref[:, :512], own[...]) + dot(right_ref[:, 512:], pair[...])
    blocks = total.astype(BF16).reshape(32, 16, 256)
    out_ref[:, 0] = blocks
    out_ref[:, 1] = blocks


def coeff_kernel(where_ref, right_ref, own, pair, out_ref):
    coefficients_of(right_ref, own, pair, out_ref)


def coeff_first_kernel(where_ref, *refs):
    parts, own, pair, out_ref, right_ref = refs[:8], *refs[8:]
    quarter, core, x_at = where_ref[0], where_ref[1], where_ref[3]
    for b in range(2):
        for u in range(4):
            r = (b ^ core) * 4 + (u ^ x_at)
            for t in range(4):
                start = pl.multiple_of((quarter ^ t) * 256, 256)
                right_ref[pl.ds(pl.multiple_of(r * 64, 64), 64), t * 256 : t * 256 + 256] = parts[b * 4 + u][
                    :, pl.ds(start, 256)
                ]
    coefficients_of(right_ref, own, pair, out_ref)


def near_inner(pieces, near_ref, out_ref):
    own, pair, inner, outer = pieces
    total = dot(near_ref[1, :, :512], own[...]) + dot(near_ref[1, :, 512:], pair[...])
    total = total + dot(near_ref[0, :, 512:], inner[...])
    out_ref[...] = total + dot(near_ref[2, :, 512:], outer[...])


def near_first_kernel(where_ref, *refs):
    pieces, parts, num, (out_ref, near_ref) = refs[:6], refs[6:14], refs[14], refs[15:]
    quarter, block, odd = where_ref[0], where_ref[2], where_ref[4]
    for half in range(2):
        for s in range(4):
            rows = pl.ds(pl.multiple_of(half * 256 + (block ^ s) * 64, 64), 64)
            for side, o in enumerate((2 - 2 * odd, 1, 2 * odd)):
                for t in range(4):
                    start = pl.multiple_of((quarter ^ t) * 256, 256)
                    near_ref[side, rows, t * 256 : t * 256 + 256] = parts[half * 4 + s][o, :, pl.ds(start, 256)]
    own, pair, inner, outer, across, beyond = pieces
    total = None
    for side, (low, high) in enumerate(((across, inner), (own, pair), (beyond, outer))):
        term = dot(near_ref[side, :, :512], low[...]) + dot(near_ref[side, :, 512:], high[...])
        total = term if total is None else total + term
    out_ref[...] = num[...] - total


def near_kernel(where_ref, own, pair, inner, outer, near_ref, out_ref):
    near_inner((own, pair, inner, outer), near_ref, out_ref)


def left_kernel(where_ref, own, received, out_ref):
    out_ref[:256] = own[...].T
    out_ref[256:] = received[...].T


def raise_kernel(where_ref, log, own, theirs):
    own[...] = jnp.exp(log[pl.ds(pl.multiple_of(where_ref[1] * 256, 256), 256), :]).astype(BF16)
    theirs[...] = jnp.exp(log[pl.ds(pl.multiple_of(256 - where_ref[1] * 256, 256), 256), :]).astype(BF16)


def join_kernel(where_ref, own, received, out_ref):
    out_ref[:256] = own[...].T
    out_ref[256:] = received[...].T


def prepare_first_kernel(where_ref, *refs):
    whole, received, (log_ref, effect_ref, load_ref, num, den, mid_state, sum_state) = refs[:4], refs[4:8], refs[8:]
    mine = pl.ds(pl.multiple_of(where_ref[1] * 256, 256), 256)
    for half in range(2):
        rows = slice(half * 256, half * 256 + 256)
        log, state, effect, load = (
            (received[i] if half else whole[i])[mine, :].T for i in range(4)
        )
        velocity = jnp.exp(log)
        state_rate = jnp.exp(-state) - velocity
        log_ref[rows] = log
        effect_ref[rows] = effect
        load_ref[rows] = load
        num[rows] = load - state_rate
        den[rows] = effect + damping * velocity
        mid_state[rows] = state + step_length * state_rate
        sum_state[rows] = state + 0.5 * step_length * state_rate


def prepare_second_kernel(where_ref, log, state, effect, load, sum_state, num, den, own, other):
    place = pl.ds(pl.multiple_of(where_ref[1] * 256, 256), 256)
    for half in range(2):
        rows = slice(half * 256, half * 256 + 256)
        velocity = jnp.exp(log[rows])
        state_rate = jnp.exp(-state[rows]) - velocity
        num[rows] = load[rows] - state_rate
        den[rows] = effect[rows] + damping * velocity
        new_state = (sum_state[rows] + 0.5 * step_length * state_rate).T
        if half:
            other[...] = new_state
        else:
            own[place, :] = new_state


def near_outer_kernel(where_ref, num, partial, across, beyond, near_ref, out_ref):
    near = partial[...] + dot(near_ref[0, :, :512], across[...]) + dot(near_ref[2, :, :512], beyond[...])
    out_ref[...] = num[...] - near


def far_first_kernel(where_ref, coeff, left, num, den, log, mid_log, sum_log, slip):
    for half in range(2):
        rows = slice(half * 256, half * 256 + 256)
        change = (num[rows] - dot(left[rows], coeff[...])) / den[rows]
        middle = log[rows] + step_length * change
        mid_log[rows] = middle
        sum_log[rows] = log[rows] + 0.5 * step_length * change
        slip[rows] = jnp.exp(middle).astype(BF16)


def far_second_kernel(where_ref, coeff, left, num, den, sum_log, own, other):
    place = pl.ds(pl.multiple_of(where_ref[1] * 256, 256), 256)
    for half in (1, 0):
        rows = slice(half * 256, half * 256 + 256)
        change = (num[rows] - dot(left[rows], coeff[...])) / den[rows]
        result = (sum_log[rows] + 0.5 * step_length * change).T
        if half:
            other[...] = result
        else:
            own[place, :] = result


def on_device(
    slip_log, fault_state, direct_effect, loading, dense_near, low_left, low_right, block_ranks
):
    row, chip, core = (lax.axis_index(name) for name in ALL)
    col = chip * 2 + core
    block, quarter = col // 4, col % 4
    x_at, z_at = row % 4, chip % 4
    where = jnp.stack([quarter, core, block, x_at, block % 2]).astype(jnp.int32)
    partner = lambda d: d ^ 1
    zl = lambda d: d ^ 2

    fourths = low_right.reshape(4, 4, 16, 1024)
    along = [pick(fourths, z_at ^ t, 1) for t in range(4)]
    along = [along[0]] + [move(along[t], lambda d: d ^ (2 * t)) for t in range(1, 4)]

    def right_target(d, u):
        r, c = d // 16, d % 16
        return ((c // 8) * 4 + ((r % 4) ^ u)) * 16 + (c % 2) * 8 + (c // 2 % 4) * 2 + r // 4

    arrived = [
        move(lax.select_n(z_at ^ x_at ^ u, *along), functools.partial(right_target, u=u)).reshape(64, 1024)
        for u in range(4)
    ]
    right_parts = arrived + [move(arrived[u], partner) for u in range(4)]

    levels = jnp.arange(32, dtype=jnp.int32)
    rows_of = row * 4 + jnp.arange(4, dtype=jnp.int32)
    cols_of = col * 2 + jnp.arange(2, dtype=jnp.int32)
    distance = jnp.abs(rows_of[:, None] - cols_of[None, :])
    far = jnp.minimum(distance, 32 - distance) > 1
    keep = ((levels < block_ranks[:, :, None]) & far[:, :, None]).reshape(4, 1, 64, 1)
    left_out = low_left.reshape(4, 64, 4, 256).transpose(0, 2, 1, 3)
    left_out = jnp.where(keep, left_out, 0).astype(BF16).reshape(16, 64, 256)
    left = lax.all_to_all(left_out, ("chip", "core"), 0, 0).reshape(1024, 256)
    lefts = (left, move(left, partner))

    def near_target(d, s):
        r, a, q = d // 16, (d % 16) // 4, d % 4
        return r * 16 + (q ^ s) * 4 + a

    parts = [move(pick(dense_near, quarter ^ s), functools.partial(near_target, s=s)) for s in range(4)]
    parts = parts + [move(parts[s], partner) for s in range(4)]

    own, theirs = call(raise_kernel, [HALF, HALF], where, (slip_log,), "raise", 1)
    (slip,) = call(join_kernel, [SLIP], where, (own, move(theirs, partner)), "join", 1)
    arrays = (slip_log, fault_state, direct_effect, loading)
    received = [move(v, partner) for v in arrays]

    def exchange(slip):
        pair = move(slip, zl)
        inner = move(slip, lambda d: d ^ 6)
        outer = move(slip, lambda d: ((d + 4 if d & 4 else d - 4) % COUNT) ^ 2)
        return (slip, pair, inner, outer), (move(pair, lambda d: d ^ 6), move(outer, zl))

    def all_to_all(sent):
        return lax.all_to_all(sent.reshape(64, 16, 256), ("row", "chip"), 0, 0).reshape(1024, 256)

    def restored(own, other):
        return lax.dynamic_update_slice(own, move(other, partner), ((1 - core) * 256, 0))

    pieces, crossed = exchange(slip)
    sent, right = call(coeff_first_kernel, [SENT, RIGHT], where, (*right_parts, *pieces[:2]), "coeff_first", 1 << 28)
    coeff = all_to_all(sent)
    (left,) = call(left_kernel, [LEFT], where, lefts, "left", 1 << 20)
    log, effect, load, num, den, mid_state, sum_state = call(
        prepare_first_kernel, [STATE] * 7, where, (*arrays, *received), "prepare_first", 1
    )
    num, near = call(near_first_kernel, [STATE, NEAR], where, (*pieces, *crossed, *parts, num), "near_first", 3 << 28)
    mid_log, sum_log, slip = call(
        far_first_kernel, [STATE, STATE, SLIP], where, (coeff, left, num, den, log), "far_first", 1 << 28
    )

    pieces, crossed = exchange(slip)
    (sent,) = call(coeff_kernel, [SENT], where, (right, *pieces[:2]), "coeff", 1 << 28)
    coeff = all_to_all(sent)
    (partial,) = call(near_kernel, [STATE], where, (*pieces, near), "near", 2 << 28)
    num, den, own, other = call(
        prepare_second_kernel, [STATE, STATE, STATE, TURNED], where,
        (mid_log, mid_state, effect, load, sum_state), "prepare_second", 1,
    )
    (num,) = call(near_outer_kernel, [STATE], where, (num, partial, *crossed, near), "near_outer", 1 << 28)
    new_state = restored(own, other)
    own, other = call(
        far_second_kernel, [STATE, TURNED], where, (coeff, left, num, den, sum_log), "far_second", 1 << 28
    )
    return restored(own, other), new_state


def solution(mesh):
    chips = Mesh(mesh.devices.reshape(8, 8, 2), ALL)
    cells, columns = P(None, ALL), ("chip", "core")
    in_specs = (
        cells, cells, cells, cells,
        P("row", None, columns, None), P("row", columns, None, None), P("row", columns, None, None), P("row", columns),
    )
    return jax.shard_map(
        on_device, mesh=chips, in_specs=in_specs, out_specs=(cells, cells), check_vma=False
    )
```

```python
import functools
import jax
import jax.numpy as jnp
from jax import lax
from jax.experimental import pallas as pl
from jax.experimental.pallas import tpu as pltpu
from jax.sharding import Mesh, PartitionSpec as P

step_length = 0.25
damping = 0.5
ALL = ("row", "chip", "core")
F32 = jnp.float32
BF16 = jnp.bfloat16
COUNT = 128


def pick(array, index, axis=0):
    return lax.dynamic_index_in_dim(array, index, axis, keepdims=False)


def move(value, target):
    return lax.ppermute(value, ALL, [(d, target(d)) for d in range(COUNT)])


def dot(a, b):
    return jnp.dot(a, b, preferred_element_type=F32)


def shape(*dims, dtype=F32):
    return jax.ShapeDtypeStruct(dims, dtype)


STATE = shape(512, 256)
SLIP = shape(512, 256, dtype=BF16)
TURNED = shape(256, 256)
HALF = shape(256, 256, dtype=BF16)
QUARTER = shape(4, 16, 1024, dtype=BF16)
LEFT = shape(512, 1024, dtype=BF16)
SENT = shape(32, 2, 16, 256, dtype=BF16)
RIGHT = shape(512, 1024, dtype=BF16)
NEAR = shape(3, 512, 1024, dtype=BF16)
SCALARS = pl.BlockSpec(memory_space=pltpu.SMEM)
VECTORS = pl.BlockSpec(memory_space=pltpu.VMEM)


SMALL = ("choose", "coeff", "near", "near_outer", "raise", "join")


def call(kernel, outs, where, operands, name, flops, scratch=()):
    return pl.pallas_call(
        kernel,
        out_shape=outs,
        in_specs=[SCALARS] + [VECTORS] * len(operands),
        out_specs=[VECTORS] * len(outs),
        scratch_shapes=scratch,
        compiler_params=pltpu.CompilerParams(vmem_limit_bytes=20 << 20) if name in SMALL else None,
        cost_estimate=pl.CostEstimate(flops=flops, bytes_accessed=5 << 20, transcendentals=0),
    )(where, *operands)


def coefficients_of(right_ref, own, pair, out_ref):
    total = dot(right_ref[:, :512], own[...]) + dot(right_ref[:, 512:], pair[...])
    blocks = total.astype(BF16).reshape(32, 16, 256)
    out_ref[:, 0] = blocks
    out_ref[:, 1] = blocks


def coeff_kernel(where_ref, right_ref, own, pair, out_ref):
    coefficients_of(right_ref, own, pair, out_ref)


def coeff_first_kernel(where_ref, *refs):
    parts, own, pair, out_ref, right_ref = refs[:8], *refs[8:]
    quarter, core, x_at = where_ref[0], where_ref[1], where_ref[3]
    for b in range(2):
        for u in range(4):
            r = (b ^ core) * 4 + (u ^ x_at)
            for t in range(4):
                start = pl.multiple_of((quarter ^ t) * 256, 256)
                right_ref[pl.ds(pl.multiple_of(r * 64, 64), 64), t * 256 : t * 256 + 256] = parts[b * 4 + u][
                    :, pl.ds(start, 256)
                ]
    coefficients_of(right_ref, own, pair, out_ref)


def near_inner(pieces, near_ref, out_ref):
    own, pair, inner, outer = pieces
    total = dot(near_ref[1, :, :512], own[...]) + dot(near_ref[1, :, 512:], pair[...])
    total = total + dot(near_ref[0, :, 512:], inner[...])
    out_ref[...] = total + dot(near_ref[2, :, 512:], outer[...])


def near_first_kernel(where_ref, *refs):
    pieces, parts, num, (out_ref, near_ref) = refs[:6], refs[6:14], refs[14], refs[15:]
    quarter, block, odd = where_ref[0], where_ref[2], where_ref[4]
    for half in range(2):
        for s in range(4):
            rows = pl.ds(pl.multiple_of(half * 256 + (block ^ s) * 64, 64), 64)
            for side, o in enumerate((2 - 2 * odd, 1, 2 * odd)):
                for t in range(4):
                    start = pl.multiple_of((quarter ^ t) * 256, 256)
                    near_ref[side, rows, t * 256 : t * 256 + 256] = parts[half * 4 + s][o, :, pl.ds(start, 256)]
    own, pair, inner, outer, across, beyond = pieces
    total = None
    for side, (low, high) in enumerate(((across, inner), (own, pair), (beyond, outer))):
        term = dot(near_ref[side, :, :512], low[...]) + dot(near_ref[side, :, 512:], high[...])
        total = term if total is None else total + term
    out_ref[...] = num[...] - total


def near_kernel(where_ref, own, pair, inner, outer, near_ref, out_ref):
    near_inner((own, pair, inner, outer), near_ref, out_ref)


def left_kernel(where_ref, own, received, out_ref):
    out_ref[:256] = own[...].T
    out_ref[256:] = received[...].T


def choose_kernel(where_ref, *refs):
    for u in range(4):
        for t in range(4):
            @pl.when(where_ref[5] == (u ^ t))
            def _(u=u, t=t):
                refs[4 + u][...] = refs[t][...]


def mask_kernel(where_ref, ranks_ref, left, out_ref):
    level = lax.broadcasted_iota(jnp.int32, (32, 256), 0)
    for i in range(4):
        for j in range(2):
            distance = jnp.abs(where_ref[6] * 4 + i - (where_ref[7] * 2 + j))
            far = jnp.minimum(distance, 32 - distance) > 1
            rank = jnp.where(far, ranks_ref[i, j], 0)
            for q in range(4):
                kept = left[i, j, :, q * 256 : q * 256 + 256].astype(F32)
                out_ref[i * 4 + q, j * 32 : j * 32 + 32, :] = jnp.where(level < rank, kept, 0.0).astype(BF16)


def raise_kernel(where_ref, log, own, theirs):
    own[...] = jnp.exp(log[pl.ds(pl.multiple_of(where_ref[1] * 256, 256), 256), :]).astype(BF16)
    theirs[...] = jnp.exp(log[pl.ds(pl.multiple_of(256 - where_ref[1] * 256, 256), 256), :]).astype(BF16)


def join_kernel(where_ref, own, received, out_ref):
    out_ref[:256] = own[...].T
    out_ref[256:] = received[...].T


def prepare_first_kernel(where_ref, *refs):
    whole, received, (log_ref, effect_ref, load_ref, num, den, mid_state, sum_state) = refs[:4], refs[4:8], refs[8:]
    mine = pl.ds(pl.multiple_of(where_ref[1] * 256, 256), 256)
    for half in range(2):
        rows = slice(half * 256, half * 256 + 256)
        log, state, effect, load = (
            (received[i] if half else whole[i])[mine, :].T for i in range(4)
        )
        velocity = jnp.exp(log)
        state_rate = jnp.exp(-state) - velocity
        log_ref[rows] = log
        effect_ref[rows] = effect
        load_ref[rows] = load
        num[rows] = load - state_rate
        den[rows] = effect + damping * velocity
        mid_state[rows] = state + step_length * state_rate
        sum_state[rows] = state + 0.5 * step_length * state_rate


def prepare_second_kernel(where_ref, log, state, effect, load, sum_state, num, den, own, other):
    place = pl.ds(pl.multiple_of(where_ref[1] * 256, 256), 256)
    for half in range(2):
        rows = slice(half * 256, half * 256 + 256)
        velocity = jnp.exp(log[rows])
        state_rate = jnp.exp(-state[rows]) - velocity
        num[rows] = load[rows] - state_rate
        den[rows] = effect[rows] + damping * velocity
        new_state = (sum_state[rows] + 0.5 * step_length * state_rate).T
        if half:
            other[...] = new_state
        else:
            own[place, :] = new_state


def near_outer_kernel(where_ref, num, partial, across, beyond, near_ref, out_ref):
    near = partial[...] + dot(near_ref[0, :, :512], across[...]) + dot(near_ref[2, :, :512], beyond[...])
    out_ref[...] = num[...] - near


def far_first_kernel(where_ref, coeff, left, num, den, log, mid_log, sum_log, slip):
    for half in range(2):
        rows = slice(half * 256, half * 256 + 256)
        change = (num[rows] - dot(left[rows], coeff[...])) / den[rows]
        middle = log[rows] + step_length * change
        mid_log[rows] = middle
        sum_log[rows] = log[rows] + 0.5 * step_length * change
        slip[rows] = jnp.exp(middle).astype(BF16)


def far_second_kernel(where_ref, coeff, left, num, den, sum_log, own, other):
    place = pl.ds(pl.multiple_of(where_ref[1] * 256, 256), 256)
    for half in (1, 0):
        rows = slice(half * 256, half * 256 + 256)
        change = (num[rows] - dot(left[rows], coeff[...])) / den[rows]
        result = (sum_log[rows] + 0.5 * step_length * change).T
        if half:
            other[...] = result
        else:
            own[place, :] = result


def on_device(
    slip_log, fault_state, direct_effect, loading, dense_near, low_left, low_right, block_ranks
):
    row, chip, core = (lax.axis_index(name) for name in ALL)
    col = chip * 2 + core
    block, quarter = col // 4, col % 4
    x_at, z_at = row % 4, chip % 4
    where = jnp.stack([quarter, core, block, x_at, block % 2, z_at ^ x_at, row, col]).astype(jnp.int32)
    partner = lambda d: d ^ 1
    zl = lambda d: d ^ 2

    fourths = low_right.reshape(4, 4, 16, 1024)
    along = [pick(fourths, z_at ^ t, 1) for t in range(4)]
    along = [along[0]] + [move(along[t], lambda d: d ^ (2 * t)) for t in range(1, 4)]

    def right_target(d, u):
        r, c = d // 16, d % 16
        return ((c // 8) * 4 + ((r % 4) ^ u)) * 16 + (c % 2) * 8 + (c // 2 % 4) * 2 + r // 4

    chosen = call(choose_kernel, [QUARTER] * 4, where, along, "choose", 1)
    arrived = [move(chosen[u], functools.partial(right_target, u=u)).reshape(64, 1024) for u in range(4)]
    right_parts = arrived + [move(arrived[u], partner) for u in range(4)]

    left_out = pl.pallas_call(
        mask_kernel,
        out_shape=shape(16, 64, 256, dtype=BF16),
        in_specs=[SCALARS, SCALARS, VECTORS],
        out_specs=VECTORS,
        compiler_params=pltpu.CompilerParams(vmem_limit_bytes=20 << 20),
        name="mask",
    )(where, block_ranks, low_left)
    left = lax.all_to_all(left_out, ("chip", "core"), 0, 0).reshape(1024, 256)
    lefts = (left, move(left, partner))

    def near_target(d, s):
        r, a, q = d // 16, (d % 16) // 4, d % 4
        return r * 16 + (q ^ s) * 4 + a

    parts = [move(pick(dense_near, quarter ^ s), functools.partial(near_target, s=s)) for s in range(4)]
    parts = parts + [move(parts[s], partner) for s in range(4)]

    own, theirs = call(raise_kernel, [HALF, HALF], where, (slip_log,), "raise", 1)
    (slip,) = call(join_kernel, [SLIP], where, (own, move(theirs, partner)), "join", 1)
    arrays = (slip_log, fault_state, direct_effect, loading)
    received = [move(v, partner) for v in arrays]

    def exchange(slip):
        pair = move(slip, zl)
        inner = move(slip, lambda d: d ^ 6)
        outer = move(slip, lambda d: ((d + 4 if d & 4 else d - 4) % COUNT) ^ 2)
        return (slip, pair, inner, outer), (move(pair, lambda d: d ^ 6), move(outer, zl))

    def all_to_all(sent):
        return lax.all_to_all(sent.reshape(64, 16, 256), ("row", "chip"), 0, 0).reshape(1024, 256)

    def restored(own, other):
        return lax.dynamic_update_slice(own, move(other, partner), ((1 - core) * 256, 0))

    pieces, crossed = exchange(slip)
    sent, right = call(coeff_first_kernel, [SENT, RIGHT], where, (*right_parts, *pieces[:2]), "coeff_first", 1 << 28)
    coeff = all_to_all(sent)
    (left,) = call(left_kernel, [LEFT], where, lefts, "left", 1 << 20)
    log, effect, load, num, den, mid_state, sum_state = call(
        prepare_first_kernel, [STATE] * 7, where, (*arrays, *received), "prepare_first", 1
    )
    num, near = call(near_first_kernel, [STATE, NEAR], where, (*pieces, *crossed, *parts, num), "near_first", 3 << 28)
    mid_log, sum_log, slip = call(
        far_first_kernel, [STATE, STATE, SLIP], where, (coeff, left, num, den, log), "far_first", 1 << 28
    )

    pieces, crossed = exchange(slip)
    (sent,) = call(coeff_kernel, [SENT], where, (right, *pieces[:2]), "coeff", 1 << 28)
    coeff = all_to_all(sent)
    (partial,) = call(near_kernel, [STATE], where, (*pieces, near), "near", 2 << 28)
    num, den, own, other = call(
        prepare_second_kernel, [STATE, STATE, STATE, TURNED], where,
        (mid_log, mid_state, effect, load, sum_state), "prepare_second", 1,
    )
    (num,) = call(near_outer_kernel, [STATE], where, (num, partial, *crossed, near), "near_outer", 1 << 28)
    new_state = restored(own, other)
    own, other = call(
        far_second_kernel, [STATE, TURNED], where, (coeff, left, num, den, sum_log), "far_second", 1 << 28
    )
    return restored(own, other), new_state


def solution(mesh):
    chips = Mesh(mesh.devices.reshape(8, 8, 2), ALL)
    cells, columns = P(None, ALL), ("chip", "core")
    in_specs = (
        cells, cells, cells, cells,
        P("row", None, columns, None), P("row", columns, None, None), P("row", columns, None, None), P("row", columns),
    )
    return jax.shard_map(
        on_device, mesh=chips, in_specs=in_specs, out_specs=(cells, cells), check_vma=False
    )
```
